256 devices in a mesh: gx: 32 (over y_hi, z, core), az: 8 (over y_lo, x).
Axes of the slice: x: 4, y: 4 (y_hi: 2, y_lo: 2; y = y_hi * 2 + y_lo), z: 8, core: 2. Of those that a mesh axis runs over, the one named last changes fastest.
Arguments:
- state: float32 [5, 512, 256, 512], P(None, 'gx', 'az'), as said below
- sponge_level: int32 [512, 256, 512], P('gx', 'az'), may hold values from 0 to 3
- inv_dx: float32 [512], P('gx'), may hold values from 1 to 8
- inv_dr: float32 [512], replicated, may hold values from 1 to 8
- target: float32 [5, 512], replicated, may hold values from -4 to 4
- cutoff: int32 [32], replicated, may hold values from 2 to 32, as said below
Outputs:
- section_state: float32 [5, 512, 256, 512], P(None, 'gx', 'az')
The draws below stay inside these ranges and needn't reach their ends.
Inputs may be any that keep to these rules, and one draw needn't show every extreme that they name: `cutoff`: every value from 2 to 32 may occur; both ends occur on some cycle. `state`: density lies between 0.7 and 1.3 and pressure is positive.
All inputs are finite; a program needn't handle non-finite values.
Results may differ from the reference program's by a relative error of at most 0.0003.
Values sent between devices are 32-bit elements; how exact they have to be, the bound alone decides.
A program may use at most 128 MiB of HBM per device.

```python
import math
import jax
import jax.numpy as jnp
from jax import lax

NT = 256
NR = 512
CYCLE = 32
PL_DEV = 16
NX = 512


def draw_state(key, part):
    keys = jax.random.split(key, 5)
    shape = (NX, NT, NR)
    noise_a = jnp.clip(jax.random.normal(keys[0], shape, jnp.float32), -4.0, 4.0)
    noise_b = jnp.clip(jax.random.normal(keys[1], shape, jnp.float32), -4.0, 4.0)
    noise_c = jnp.clip(jax.random.normal(keys[2], shape, jnp.float32), -4.0, 4.0)
    density = 0.7 + 0.6 * jax.random.uniform(keys[3], shape, jnp.float32)
    pressure = 0.7 + 0.6 * jax.random.uniform(keys[4], shape, jnp.float32)
    axial_momentum = density * (0.9 + 0.3 * noise_a)
    radial_momentum = 0.3 * noise_b
    swirl_momentum = 0.3 * noise_c
    energy = pressure / 0.4 + 0.5 * (axial_momentum * axial_momentum + radial_momentum * radial_momentum + swirl_momentum * swirl_momentum) / density
    return jnp.stack([density, axial_momentum, radial_momentum, swirl_momentum, energy]).astype(jnp.float32)


def draw_cutoff(key, part):
    keys = jax.random.split(key, 3)
    highest = NT // 8
    values = jax.random.randint(keys[0], (CYCLE,), 2, highest + 1)
    first_cycle = jax.random.randint(keys[1], (), 0, CYCLE)
    second_cycle = (first_cycle + jax.random.randint(keys[2], (), 1, CYCLE)) % CYCLE
    values = values.at[first_cycle].set(highest).at[second_cycle].set(2)
    return values.astype(jnp.int32)


def with_ends(drawn, key, low, top_value):
    index_at = [jax.random.randint(jax.random.fold_in(key, axis), (), 0, length) for axis, length in enumerate(drawn.shape)]
    longest = drawn.shape.index(max(drawn.shape))
    neighbour = index_at[:longest] + [(index_at[longest] + 1) % drawn.shape[longest]] + index_at[longest + 1:]
    return drawn.at[tuple(index_at)].set(low).at[tuple(neighbour)].set(top_value)


def steps_of(key, extent, cuts, low, largest):
    def one(axis_at, parts):
        steps = jax.random.uniform(jax.random.fold_in(jax.random.fold_in(key, 6), axis_at), (parts,), jnp.float32, low / len(cuts), largest / len(cuts))
        return jnp.repeat(jnp.exp(steps), extent[axis_at] // parts).reshape((-1,) + (1,) * (len(extent) - axis_at - 1))

    gain = one(*cuts[0])
    for cut in cuts[1:]:
        gain = gain * one(*cut)
    return gain


def noise(stream_key, extent, scale, reach, kind=jnp.bfloat16):
    result = scale * jax.random.normal(stream_key, extent, jnp.float32)
    return jnp.clip(result, min=-reach, max=reach).astype(kind)


def setup_inputs(seed: int = 0) -> dict:
    splits = jax.random.split(jax.random.key(seed), 7)
    state = draw_state(jax.random.fold_in(splits[6], 71), 0)
    sponge_level = with_ends(jax.random.randint(splits[1], (NX, NT, NR), 0, 4), jax.random.fold_in(splits[1], 1), 0, 3).astype(jnp.int32)
    inv_dx = jnp.clip(jnp.exp(math.log(8.0) - 2.0794415 * jax.random.uniform(splits[2], (NX,), jnp.float32) ** steps_of(splits[2], (NX,), ((0, 32),), -0.2, 0.2)), 1.0, 8.0)
    inv_dr = jnp.clip(jnp.exp(jax.random.uniform(splits[3], (NR,), jnp.float32, math.log(1.0), math.log(8.0))), 1.0, 8.0)
    target = noise(splits[4], (5, NR), 1.0, 4.0, jnp.float32)
    cutoff = draw_cutoff(jax.random.fold_in(splits[6], 71), 0)
    return {"state": state, "sponge_level": sponge_level, "inv_dx": inv_dx, "inv_dr": inv_dr, "target": target, "cutoff": cutoff}


gas_factor = 0.4
time_step = 0.02
sponge_rate = 4.0


def cycle_radius(length):
    return 1.0 + 4.0 * jnp.arange(length, dtype=jnp.float32) / length


def flux_parts(fields, radius):
    density = fields[0]
    axial_momentum = fields[1]
    radial_momentum = fields[2]
    swirl_momentum = fields[3]
    energy = fields[4]
    axial_speed = axial_momentum / density
    radial_speed = radial_momentum / density
    swirl_speed = swirl_momentum / density
    pressure = gas_factor * (energy - 0.5 * (axial_momentum * axial_speed + radial_momentum * radial_speed + swirl_momentum * swirl_speed))
    enthalpy = energy + pressure
    axial_flux = jnp.stack([axial_momentum, axial_momentum * axial_speed + pressure, radial_momentum * axial_speed, swirl_momentum * axial_speed, enthalpy * axial_speed])
    radial_flux = radius * jnp.stack([radial_momentum, axial_momentum * radial_speed, radial_momentum * radial_speed + pressure, swirl_momentum * radial_speed, enthalpy * radial_speed])
    swirl_flux = jnp.stack([swirl_momentum, axial_momentum * swirl_speed, radial_momentum * swirl_speed, swirl_momentum * swirl_speed + pressure, enthalpy * swirl_speed])
    press_source = (pressure + swirl_momentum * swirl_speed) / radius
    turn_source = -(radial_momentum * swirl_speed) / radius
    return axial_flux, radial_flux, swirl_flux, press_source, turn_source


def reference(state, sponge_level, inv_dx, inv_dr, target, cutoff):
    block_total = NX // PL_DEV
    radius = cycle_radius(NR)
    mode_index = jnp.arange(NT // 2 + 1, dtype=jnp.int32)
    kept_modes = (mode_index[:, None] <= cutoff[None, :]).astype(jnp.float32)

    def one_block(block_index):
        offset = block_index * PL_DEV
        plane_index = offset - 1 + jnp.arange(PL_DEV + 2, dtype=jnp.int32)
        inside_grid = (plane_index >= 0) & (plane_index < NX)
        clipped = jnp.clip(plane_index, 0, NX - 1).astype(jnp.int32)
        slab_state = jnp.take(state, clipped, axis=1)
        axial_flux, radial_flux, swirl_flux, press_source, turn_source = flux_parts(slab_state, radius)
        axial_flux = jnp.where(inside_grid[None, :, None, None], axial_flux, 0.0)
        own_state = slab_state[:, 1:-1]
        radial_flux = radial_flux[:, 1:-1]
        swirl_flux = swirl_flux[:, 1:-1]
        press_source = press_source[1:-1]
        turn_source = turn_source[1:-1]
        scale_x = lax.dynamic_slice_in_dim(inv_dx, offset.astype(jnp.int32), PL_DEV, 0)
        levels = lax.dynamic_slice_in_dim(sponge_level, offset.astype(jnp.int32), PL_DEV, 0)
        axial_term = (axial_flux[:, 2:] - axial_flux[:, :-2]) * (0.5 * scale_x)[None, :, None, None]
        radial_pad = jnp.pad(radial_flux, ((0, 0), (0, 0), (0, 0), (1, 1)))
        radial_term = (radial_pad[..., 2:] - radial_pad[..., :-2]) * (0.5 * inv_dr / radius)
        swirl_term = (jnp.roll(swirl_flux, -1, axis=2) - jnp.roll(swirl_flux, 1, axis=2)) * ((NT / (4.0 * jnp.pi)) / radius)
        tendency = -(axial_term + radial_term + swirl_term)
        zero_field = jnp.zeros_like(press_source)
        tendency = tendency + jnp.stack([zero_field, zero_field, press_source, turn_source, zero_field])
        tendency = tendency - sponge_rate * levels.astype(jnp.float32)[None] * (own_state - target[:, None, None, :])
        updated = own_state + time_step * tendency
        inner_block = updated[..., :CYCLE]
        spectrum = jnp.fft.rfft(inner_block, axis=2)
        filtered = jnp.fft.irfft(spectrum * kept_modes[None, None], n=NT, axis=2).astype(updated.dtype)
        return jnp.concatenate([filtered, updated[..., CYCLE:]], axis=3)

    blocks = lax.map(one_block, jnp.arange(block_total, dtype=jnp.int32))
    return jnp.moveaxis(blocks, 0, 1).reshape(5, NX, NT, NR)
```

```python
import jax
import jax.numpy as jnp
import numpy as np
from jax import lax
from jax.experimental import pallas as pl
from jax.experimental.pallas import tpu as pltpu
from jax.sharding import PartitionSpec as P

NT = 256
CYCLE = 32
NR = 512
PL_DEV = 16
CELLS = 32
TOP = 32
LT = NR // 128

time_step = 0.02
sponge_rate = 4.0

ROWS = 88
BACK = 80


def tables():
    cell = np.arange(NT)
    cos = np.cos(2 * np.pi * ((np.arange(TOP + 1)[:, None] * cell[None]) % NT) / NT)
    sin = np.sin(2 * np.pi * ((np.arange(1, TOP + 1)[:, None] * cell[None]) % NT) / NT)
    whole = np.zeros((80, NT), np.float32)
    whole[: TOP + 1] = cos
    whole[TOP + 1 : 2 * TOP + 1] = sin
    high = whole.astype(jnp.bfloat16)
    low = (whole - high.astype(np.float32)).astype(jnp.bfloat16)
    fwd = np.concatenate([high, low], 0)
    inv = np.concatenate([high.T, low.T, high.T], 1)
    return fwd, inv


def prims(st):
    density, mx, mr, ms, energy = st
    inv = 1.0 / density
    u = mx * inv
    v = mr * inv
    w = ms * inv
    a = mx * u
    b = mr * v
    c = ms * w
    pressure = 0.4 * (energy - 0.5 * (a + b + c))
    return u, v, w, a, b, c, pressure, energy + pressure


def kernel(
    state, sponge, inv_dr, target, fwd_t, inv_t, inv_dx, cutoff, out,
    ST, FX, PART, SP, TG, IDR, CC, TT, LC, SB, RB, SB2, R2, WT,
    load_sem, small_sem, ax_send, ax_recv, sw_send, sw_recv, send1, recv1, send2, recv2,
):
    gx = lax.axis_index("gx")
    az = lax.axis_index("az")
    n_gx = lax.axis_size("gx")
    n_az = lax.axis_size("az")
    up, down = lax.rem(gx + 1, n_gx), lax.rem(gx + n_gx - 1, n_gx)
    east, west = lax.rem(az + 1, n_az), lax.rem(az + n_az - 1, n_az)

    barrier = pltpu.get_barrier_semaphore()
    for k in range(1, n_az):
        pl.semaphore_signal(barrier, inc=1, device_id={"az": lax.rem(az + k, n_az)})
    for g in (up, down):
        pl.semaphore_signal(barrier, inc=1, device_id={"gx": g})

    def lanes(l):
        return pl.ds(l * 128, 128)

    loads = []
    for l in range(LT):
        loads.append(
            (
                pltpu.make_async_copy(
                    state.at[:, :, :, lanes(l)],
                    ST.at[l, :, 1:17, 8:40, :],
                    load_sem.at[2 * l],
                ),
                pltpu.make_async_copy(
                    sponge.at[:, :, lanes(l)], SP.at[l], load_sem.at[2 * l + 1]
                ),
            )
        )
    small = [
        pltpu.make_async_copy(inv_dr, IDR, small_sem.at[0]),
        pltpu.make_async_copy(target, TG, small_sem.at[1]),
        pltpu.make_async_copy(fwd_t, CC, small_sem.at[2]),
        pltpu.make_async_copy(inv_t, TT, small_sem.at[3]),
    ]
    for c in loads[0]:
        c.start()
    small[0].start()
    small[1].start()

    def axial(l, side):
        plane = 15 if side == 0 else 0
        slot = 0 if side == 0 else 17
        return pltpu.make_async_remote_copy(
            src_ref=state.at[:, plane : plane + 1, :, lanes(l)],
            dst_ref=ST.at[l, :, slot : slot + 1, 8:40, :],
            send_sem=ax_send.at[l, side],
            recv_sem=ax_recv.at[l, side],
            device_id={"gx": up if side == 0 else down},
        )

    def swirl(l, side):
        row = 31 if side == 0 else 0
        slot = 7 if side == 0 else 40
        return pltpu.make_async_remote_copy(
            src_ref=state.at[:, :, row : row + 1, lanes(l)],
            dst_ref=ST.at[l, :, 1:17, slot : slot + 1, :],
            send_sem=sw_send.at[l, side],
            recv_sem=sw_recv.at[l, side],
            device_id={"az": east if side == 0 else west},
        )

    axials = [[axial(l, s) for s in range(2)] for l in range(LT)]
    swirls = [[swirl(l, s) for s in range(2)] for l in range(LT)]

    lane = lax.broadcasted_iota(jnp.int32, (8, 128), 1)
    row = lax.broadcasted_iota(jnp.int32, (8, 128), 0)

    small[0].wait()
    small[1].wait()
    for l in range(LT):
        j = lane + l * 128
        jf = j.astype(jnp.float32)
        radius = 1.0 + 4.0 * jf / NR
        after = 1.0 + 4.0 * (jf + 1.0) / NR
        before = 1.0 + 4.0 * (jf - 1.0) / NR
        inv_r = 1.0 / radius
        rr = (0.5 * time_step) * jnp.broadcast_to(IDR[:, l * 128 : (l + 1) * 128], (8, 128)) * inv_r
        LC[0, l] = jnp.where(j == NR - 1, 0.0, rr * after)
        LC[1, l] = jnp.where(j == 0, 0.0, rr * before)
        LC[2, l] = (time_step * NT / (4.0 * np.pi)) * inv_r
        LC[3, l] = time_step * inv_r
        for f in range(5):
            LC[4 + f, l] = jnp.broadcast_to(TG[f : f + 1, l * 128 : (l + 1) * 128], (8, 128))

    cut = jnp.zeros((8, 128), jnp.int32)
    for j in range(CYCLE):
        cut = jnp.where((lane & (CYCLE - 1)) == j, cutoff[j], cut)
    for b in range(10):
        k = row + 8 * b
        mode = jnp.where(k > TOP, k - TOP, k)
        kept = (mode <= cut) & (k <= 2 * TOP)
        WT[8 * b : 8 * b + 8] = jnp.where(kept, jnp.where(k == 0, 1.0 / NT, 2.0 / NT), 0.0)

    zero = jnp.zeros((8, 128), jnp.float32)
    SWIRL = (7, 2, 4, 5, 6)

    def clear(p, _):
        for c in SWIRL:
            FX[0, c, p, 0:8] = zero
            FX[0, c, p, 40:48] = zero
        return 0

    lax.fori_loop(1, 17, clear, 0)
    for e in range(8):
        SB[e, 80:88] = zero

    pl.semaphore_wait(barrier, n_az + 1)
    for s in range(2):
        axials[0][s].start()
    for l in range(1, LT):
        for c in loads[l]:
            c.start()
    small[2].start()
    small[3].start()
    for l in range(1, LT):
        for s in range(2):
            axials[l][s].start()

    def axial_fluxes(l, p, r, st):
        density, mx, mr, ms, energy = st
        u, v, w, a, b, c, pressure, h = prims(st)
        FX[l, 0, p, r] = a + pressure
        a2 = mr * u
        FX[l, 1, p, r] = a2
        FX[l, 2, p, r] = ms * u
        FX[l, 3, p, r] = h * u
        return v, w, b, c, pressure, h, a2

    def swirl_fluxes(l, p, r, mr, ms, w, c, pressure, h):
        s2 = mr * w
        s3 = c + pressure
        FX[l, 4, p, r] = s2
        FX[l, 5, p, r] = s3
        FX[l, 6, p, r] = h * w
        FX[l, 7, p, r] = ms
        return s2, s3

    def block(ls, p, g):
        r = pl.ds(8 + 8 * g, 8)
        states, radials, sources = [], [], []
        for l in ls:
            st = [ST[l, f, p, r] for f in range(5)]
            mr, ms = st[2], st[3]
            v, w, b, c, pressure, h, a2 = axial_fluxes(l, p, r, st)
            s2, s3 = swirl_fluxes(l, p, r, mr, ms, w, c, pressure, h)
            states.append(st)
            radials.append((mr, a2, b + pressure, s2, h * v))
            sources.append((s2, s3))
        fwd = [[pltpu.roll(x, 127, 1) for x in rs] for rs in radials]
        bwd = [[pltpu.roll(x, 1, 1) for x in rs] for rs in radials]
        for i, l in enumerate(ls):
            level = SP[l, p - 1, pl.ds(8 * g, 8)].astype(jnp.float32) * (time_step * sponge_rate)
            for f in range(5):
                ahead, behind = fwd[i][f], bwd[i][f]
                if i + 1 < len(ls):
                    ahead = jnp.where(lane == 127, fwd[i + 1][f], ahead)
                if i > 0:
                    behind = jnp.where(lane == 0, bwd[i - 1][f], behind)
                x = states[i][f]
                part = x - level * (x - LC[4 + f, l]) - (ahead * LC[0, l] - behind * LC[1, l])
                if f == 2:
                    part = part + LC[3, l] * sources[i][1]
                if f == 3:
                    part = part - LC[3, l] * sources[i][0]
                PART[l, f, p - 1, pl.ds(8 * g, 8)] = part

    def edge_plane(l, p):
        for g in range(4):
            r = pl.ds(8 + 8 * g, 8)
            axial_fluxes(l, p, r, [ST[l, f, p, r] for f in range(5)])

    def second(l, f, p, g, ahead, behind):
        r = pl.ds(8 + 8 * g, 8)
        if f == 0:
            above, below = ST[l, 1, p + 1, r], ST[l, 1, p - 1, r]
        else:
            above, below = FX[l, f - 1, p + 1, r], FX[l, f - 1, p - 1, r]
        c = SWIRL[f]
        turn = FX[l, c, p, pl.ds(9 + 8 * g, 8)] - FX[l, c, p, pl.ds(7 + 8 * g, 8)]
        x = PART[l, f, p - 1, pl.ds(8 * g, 8)]
        return x - (above * ahead - below * behind) - LC[2, l] * turn

    def steps_of(p):
        step = (0.5 * time_step) * inv_dx[p - 1]
        none = jnp.float32(0.0)
        ahead = jnp.where((p == 16) & (gx == n_gx - 1), none, step)
        behind = jnp.where((p == 1) & (gx == 0), none, step)
        return ahead, behind

    def pack(xs):
        got = xs[0]
        for i in range(1, 4):
            got = jnp.where(lane >= 32 * i, pltpu.roll(xs[i], 32 * i, 1), got)
        return got

    def forth(e):
        return pltpu.make_async_remote_copy(
            src_ref=SB.at[e], dst_ref=RB.at[az], send_sem=send1.at[e], recv_sem=recv1.at[az],
            device_id={"az": e},
        )

    def group(q):
        planes = [lax.rem(1 + 4 * q + i, 16) + 1 for i in range(4)]
        coefs = [steps_of(p) for p in planes]
        for f in range(5):
            xs = [pack([second(0, f, p, g, *s) for p, s in zip(planes, coefs)]) for g in range(4)]
            c = SWIRL[f]
            first = pack([FX[0, c, p, 8:16] for p in planes]) * pack([-LC[2, 0]] * 4)
            last = pack([FX[0, c, p, 32:40] for p in planes]) * pack([LC[2, 0]] * 4)
            if f != 2:
                e = q if f < 2 else q + 4
                s = f if f < 2 else f - 3
                for g in range(4):
                    SB[e, 32 * s + 8 * g : 32 * s + 8 * g + 8] = xs[g]
                SB[e, 80 + 2 * s : 81 + 2 * s] = first[0:1]
                SB[e, 81 + 2 * s : 82 + 2 * s] = last[7:8]
            else:
                half = lane < 64
                for g in range(2):
                    SB[q, 64 + 8 * g : 72 + 8 * g] = jnp.where(half, xs[g], pltpu.roll(xs[g + 2], 64, 1))
                    SB[q + 4, 64 + 8 * g : 72 + 8 * g] = jnp.where(half, pltpu.roll(xs[g], 64, 1), xs[g + 2])
                low = lax.broadcasted_iota(jnp.int32, (1, 128), 1) < 64
                top, end = first[0:1], last[7:8]
                SB[q, 84:85] = jnp.where(low, end, pltpu.roll(first, 64, 1)[0:1])
                SB[q + 4, 84:85] = jnp.where(low, pltpu.roll(last, 64, 1)[7:8], top)
        for y in range(2):
            e = q + 4 * y

            @pl.when(e != az)
            def _():
                forth(e).start()

            @pl.when(e == az)
            def _():
                RB[e] = SB[e]

    for c in loads[0]:
        c.wait()

    def inner(p, _):
        for g in range(4):
            block([0], p, g)
        return 0

    lax.fori_loop(1, 17, inner, 0)

    def early(q, _):
        group(q)
        return 0

    lax.fori_loop(0, 3, early, 0)
    for s in range(2):
        axials[0][s].wait_recv()
    edge_plane(0, 0)
    edge_plane(0, 17)
    group(jnp.int32(3))
    for l in range(LT):
        for s in range(2):
            swirls[l][s].start()

    for l in range(1, LT):
        for c in loads[l]:
            c.wait()

    def outer(p, _):
        for g in range(4):
            block(list(range(LT)), p, g)
        return 0

    lax.fori_loop(1, 17, outer, 0)

    small[2].wait()
    small[3].wait()
    for s in range(8):

        @pl.when(s != az)
        def _():
            pltpu.make_async_remote_copy(
                src_ref=SB.at[s], dst_ref=RB.at[s], send_sem=send1.at[s], recv_sem=recv1.at[s],
                device_id={"az": jnp.int32(s)},
            ).wait_recv()

    low1 = lax.broadcasted_iota(jnp.int32, (1, 128), 1) < 64
    for d in range(8):
        prev, nxt = (d + 7) % 8, (d + 1) % 8
        for s in range(2):
            RB[d, 32 * s : 32 * s + 1] += RB[prev, 81 + 2 * s : 82 + 2 * s]
            RB[d, 32 * s + 31 : 32 * s + 32] += RB[nxt, 80 + 2 * s : 81 + 2 * s]
        RB[d, 64:65] += jnp.where(low1, RB[prev, 84:85], 0.0)
        RB[d, 79:80] += jnp.where(low1, 0.0, RB[nxt, 84:85])
    half16 = lax.broadcasted_iota(jnp.int32, (16, 128), 1) < 64
    for s in range(3):
        if s < 2:
            xs = [RB[d, 32 * s : 32 * s + 32] for d in range(8)]
        else:
            xs = []
            for d in range(8):
                t = RB[d, 64:80]
                xs += [t, pltpu.roll(t, 64, 1)]
        x = jnp.concatenate(xs, 0)
        high = x.astype(jnp.bfloat16)
        low = (x - high.astype(jnp.float32)).astype(jnp.bfloat16)
        both = jnp.dot(CC[...], high, preferred_element_type=jnp.float32)
        coef = both[0:80] + both[80:160] + jnp.dot(CC[0:80], low, preferred_element_type=jnp.float32)
        z = coef * WT[...]
        zh = z.astype(jnp.bfloat16)
        zl = (z - zh.astype(jnp.float32)).astype(jnp.bfloat16)
        y = jnp.dot(TT[...], jnp.concatenate([zh, zh, zl], 0), preferred_element_type=jnp.float32)
        for d in range(8):
            yd = y[32 * d : 32 * d + 32]
            if s < 2:
                SB2[d, 32 * s : 32 * s + 32] = yd
            else:
                SB2[d, 64:80] = jnp.where(half16, yd[0:16], pltpu.roll(yd[16:32], 64, 1))

    def back(d, src):
        return pltpu.make_async_remote_copy(
            src_ref=SB2.at[d], dst_ref=R2.at[src], send_sem=send2.at[d], recv_sem=recv2.at[src],
            device_id={"az": jnp.int32(d)},
        )

    for d in range(8):

        @pl.when(d != az)
        def _():
            back(d, az).start()

        @pl.when(d == az)
        def _():
            R2[d] = SB2[d]

    for l in range(LT):
        for s in range(2):
            if l > 0:
                axials[l][s].wait_recv()
            swirls[l][s].wait_recv()
    for l in range(1, LT):
        edge_plane(l, 0)
        edge_plane(l, 17)

    def pads(p, _):
        for l in range(LT):
            for r0 in (0, 40):
                r = pl.ds(r0, 8)
                st = [ST[l, f, p, r] for f in range(5)]
                u, v, w, a, b, c, pressure, h = prims(st)
                FX[l, 2, p, r] = st[3] * u
                swirl_fluxes(l, p, r, st[2], st[3], w, c, pressure, h)
        return 0

    lax.fori_loop(1, 17, pads, 0)

    def finish(p, _):
        ahead, behind = steps_of(p)
        for l in range(LT):
            for f in range(5):
                for g in range(4):
                    out[f, p - 1, 8 * g : 8 * g + 8, l * 128 : (l + 1) * 128] = second(l, f, p, g, ahead, behind)
        return 0

    lax.fori_loop(1, 17, finish, 0)

    for s in range(8):

        @pl.when(s != az)
        def _():
            back(s, s).wait_recv()

    def merge(q, _):
        for i in range(4):
            p = lax.rem(1 + 4 * q + i, 16)
            for f in range(5):
                for g in range(4):
                    if f != 2:
                        e = q if f < 2 else q + 4
                        s = f if f < 2 else f - 3
                        x = R2[e, 32 * s + 8 * g : 32 * s + 8 * g + 8]
                        base = 32 * i
                    else:
                        e = q if i < 2 else q + 4
                        x = R2[e, 64 + 8 * (g % 2) : 72 + 8 * (g % 2)]
                        base = 32 * (i % 2) + 64 * (g // 2)
                    if base:
                        x = pltpu.roll(x, 128 - base, 1)
                    old = out[f, p, 8 * g : 8 * g + 8, 0:128]
                    out[f, p, 8 * g : 8 * g + 8, 0:128] = jnp.where(lane < 32, x, old)
        return 0

    lax.fori_loop(0, 4, merge, 0)

    for l in range(LT):
        for s in range(2):
            axials[l][s].wait_send()
            swirls[l][s].wait_send()
    for e in range(8):

        @pl.when(e != az)
        def _():
            forth(jnp.int32(e)).wait_send()
            back(e, az).wait_send()


def solution(mesh):
    fwd, inv = tables()

    def body(state, sponge_level, inv_dx, inv_dr, target, cutoff):
        f32 = jnp.float32
        hbm = pl.BlockSpec(memory_space=pl.ANY)
        smem = pl.BlockSpec(memory_space=pltpu.SMEM)
        dma = pltpu.SemaphoreType.DMA
        return pl.pallas_call(
            kernel,
            out_shape=jax.ShapeDtypeStruct(state.shape, f32),
            in_specs=[hbm] * 6 + [smem] * 2,
            out_specs=pl.BlockSpec(memory_space=pltpu.VMEM),
            scratch_shapes=[
                pltpu.VMEM((LT, 5, 18, 48, 128), f32),
                pltpu.VMEM((LT, 8, 18, 48, 128), f32),
                pltpu.VMEM((LT, 5, 16, 32, 128), f32),
                pltpu.VMEM((LT, 16, 32, 128), jnp.int32),
                pltpu.VMEM((5, NR), f32),
                pltpu.VMEM((1, NR), f32),
                pltpu.VMEM(fwd.shape, jnp.bfloat16),
                pltpu.VMEM(inv.shape, jnp.bfloat16),
                pltpu.VMEM((9, LT, 8, 128), f32),
                pltpu.VMEM((8, ROWS, 128), f32),
                pltpu.VMEM((8, ROWS, 128), f32),
                pltpu.VMEM((8, BACK, 128), f32),
                pltpu.VMEM((8, BACK, 128), f32),
                pltpu.VMEM((80, 128), f32),
                dma((2 * LT,)),
                dma((4,)),
                dma((LT, 2)),
                dma((LT, 2)),
                dma((LT, 2)),
                dma((LT, 2)),
                dma((8,)),
                dma((8,)),
                dma((8,)),
                dma((8,)),
            ],
            compiler_params=pltpu.CompilerParams(collective_id=0, has_side_effects=True, vmem_limit_bytes=52 << 20),
        )(state, sponge_level, inv_dr.reshape(1, NR), target, jnp.asarray(fwd), jnp.asarray(inv), inv_dx, cutoff)

    return jax.shard_map(
        body,
        mesh=mesh,
        in_specs=(P(None, "gx", "az", None), P("gx", "az", None), P("gx"), P(), P(), P()),
        out_specs=P(None, "gx", "az", None),
        check_vma=False,
    )
```

```python
import jax
import jax.numpy as jnp
import numpy as np
from jax import lax
from jax.experimental import pallas as pl
from jax.experimental.pallas import tpu as pltpu
from jax.sharding import PartitionSpec as P

NT = 256
CYCLE = 32
NR = 512
PL_DEV = 16
CELLS = 32
TOP = 32
LT = NR // 128

time_step = 0.02
sponge_rate = 4.0

ROWS = 88
BACK = 80
N1 = 12


def tables():
    cell = np.arange(NT)
    cos = np.cos(2 * np.pi * ((np.arange(TOP + 1)[:, None] * cell[None]) % NT) / NT)
    sin = np.sin(2 * np.pi * ((np.arange(1, TOP + 1)[:, None] * cell[None]) % NT) / NT)
    whole = np.zeros((80, NT), np.float32)
    whole[: TOP + 1] = cos
    whole[TOP + 1 : 2 * TOP + 1] = sin
    high = whole.astype(jnp.bfloat16)
    low = (whole - high.astype(np.float32)).astype(jnp.bfloat16)
    fwd = np.concatenate([high, low], 0)
    inv = np.concatenate([high.T, low.T, high.T], 1)
    return fwd, inv


def prims(st):
    density, mx, mr, ms, energy = st
    inv = 1.0 / density
    u = mx * inv
    v = mr * inv
    w = ms * inv
    a = mx * u
    b = mr * v
    c = ms * w
    pressure = 0.4 * (energy - 0.5 * (a + b + c))
    return u, v, w, a, b, c, pressure, energy + pressure


def kernel(
    state, sponge, inv_dr, target, fwd_t, inv_t, inv_dx_in, cutoff_in, out, R2,
    ST, FX, PART, SP, TG, IDR, CC, TT, LC, PC, PI, FA, SI, SB, RB, SB2, HS, HR, RL, WT, inv_dx, cutoff,
    load_sem, small_sem, ax_send, ax_recv, sw_send, sw_recv, send1, recv1, send2, recv2, hs_send, hs_recv,
    rl_send, rl_recv,
):
    gx = lax.axis_index("gx")
    az = lax.axis_index("az")
    n_gx = lax.axis_size("gx")
    n_az = lax.axis_size("az")
    has_up, has_down = gx < n_gx - 1, gx > 0
    up, down = lax.rem(gx + 1, n_gx), lax.rem(gx + n_gx - 1, n_gx)
    east, west = lax.rem(az + 1, n_az), lax.rem(az + n_az - 1, n_az)
    partner = lax.rem(az + 4, n_az)
    mid = n_gx // 2
    up_relay = [mid - 1 - 2 * l for l in range(LT)]
    down_relay = [n_gx - 1 - 2 * l for l in range(LT)]
    first_x, last_x = lax.rem(az, 4) == 0, lax.rem(az, 4) == 3

    def lanes(l):
        return pl.ds(l * 128, 128)

    loads = []
    for l in range(LT):
        loads.append(
            (
                pltpu.make_async_copy(
                    state.at[:, :, :, lanes(l)],
                    ST.at[l, :, 1:17, 8:40, :],
                    load_sem.at[2 * l],
                ),
                pltpu.make_async_copy(
                    sponge.at[:, :, lanes(l)], SP.at[l], load_sem.at[2 * l + 1]
                ),
            )
        )
    small = [
        pltpu.make_async_copy(inv_dr, IDR, small_sem.at[0]),
        pltpu.make_async_copy(target, TG, small_sem.at[1]),
        pltpu.make_async_copy(fwd_t, CC, small_sem.at[2]),
        pltpu.make_async_copy(inv_t, TT, small_sem.at[3]),
        pltpu.make_async_copy(inv_dx_in, inv_dx, small_sem.at[4]),
        pltpu.make_async_copy(cutoff_in, cutoff, small_sem.at[5]),
    ]
    for k in (0, 1, 4, 5):
        small[k].start()
    for c in loads[0]:
        c.start()
    barrier = pltpu.get_barrier_semaphore()
    for k in range(1, n_az):
        pl.semaphore_signal(barrier, inc=1, device_id={"az": lax.rem(az + k, n_az)})
    for there, g, holds in ((has_down, down, first_x), (has_up, up, last_x)):

        @pl.when(there)
        def _():
            pl.semaphore_signal(barrier, inc=1, device_id={"gx": g})

        @pl.when(there & holds)
        def _():
            for d in range(8):
                pl.semaphore_signal(barrier, inc=1, device_id={"gx": g, "az": jnp.int32(d)})

    relays = 0
    for l in range(LT):
        for g, to in (
            (up_relay[l], mid - 1), (mid, up_relay[l]), (down_relay[l], mid), (mid - 1, down_relay[l])
        ):
            if g != to:

                @pl.when(gx == g)
                def _():
                    pl.semaphore_signal(barrier, inc=1, device_id={"gx": jnp.int32(to), "az": partner})

                relays = relays + (gx == to).astype(jnp.int32)
    greeted = n_az - 1 + 3 * has_up.astype(jnp.int32) + 3 * has_down.astype(jnp.int32) + relays


    def axial(l, side):
        plane = 15 if side == 0 else 0
        slot = 0 if side == 0 else 17
        return pltpu.make_async_remote_copy(
            src_ref=state.at[:, plane : plane + 1, :, lanes(l)],
            dst_ref=ST.at[l, :, slot : slot + 1, 8:40, :],
            send_sem=ax_send.at[l, side],
            recv_sem=ax_recv.at[l, side],
            device_id={"gx": up if side == 0 else down},
        )

    def swirl(l, side):
        row = 31 if side == 0 else 0
        slot = 7 if side == 0 else 40
        return pltpu.make_async_remote_copy(
            src_ref=state.at[:, :, row : row + 1, lanes(l)],
            dst_ref=ST.at[l, :, 1:17, slot : slot + 1, :],
            send_sem=sw_send.at[l, side],
            recv_sem=sw_recv.at[l, side],
            device_id={"az": east if side == 0 else west},
        )

    axials = [[axial(l, s) for s in range(2)] for l in range(LT)]
    swirls = [[swirl(l, s) for s in range(2)] for l in range(LT)]
    sends_to = (has_up, has_down)
    direct = (has_up & (gx != mid - 1), has_down & (gx != mid))
    gets_from = (has_down, has_up)

    lane = lax.broadcasted_iota(jnp.int32, (8, 128), 1)
    row = lax.broadcasted_iota(jnp.int32, (8, 128), 0)
    cycle = lane & (CYCLE - 1)

    def pack(xs):
        got = xs[0]
        for i in range(1, 4):
            got = jnp.where(lane >= 32 * i, pltpu.roll(xs[i], 32 * i, 1), got)
        return got

    for k in (0, 1, 4, 5):
        small[k].wait()

    def coefficients(j, spacing):
        jf = j.astype(jnp.float32)
        after = 1.0 + 4.0 * (jf + 1.0) / NR
        before = 1.0 + 4.0 * (jf - 1.0) / NR
        inv_r = 1.0 / (1.0 + 4.0 * jf / NR)
        rr = (0.5 * time_step) * spacing * inv_r
        return (
            jnp.where(j == NR - 1, 0.0, rr * after),
            jnp.where(j == 0, 0.0, rr * before),
            (time_step * NT / (4.0 * np.pi)) * inv_r,
            time_step * inv_r,
        )

    def wide(ref, f, l):
        return jnp.broadcast_to(ref[f : f + 1, l * 128 : (l + 1) * 128], (8, 128))

    for k, x in enumerate(coefficients(cycle, pack([wide(IDR, 0, 0)] * 4))):
        PC[k] = x
    for f in range(5):
        PC[4 + f] = pack([wide(TG, f, 0)] * 4)
    for q in range(4):
        x = jnp.zeros((8, 128), jnp.float32)
        for i in range(4):
            x = jnp.where(lane >= 32 * i, (0.5 * time_step) * inv_dx[4 * q + i], x)
        PC[9 + q] = x
    for l in range(LT):
        for k, x in enumerate(coefficients(lane + l * 128, wide(IDR, 0, l))):
            LC[k, l] = x
        for f in range(5):
            LC[4 + f, l] = wide(TG, f, l)

    cut = jnp.zeros((8, 128), jnp.int32)
    for j in range(CYCLE):
        cut = jnp.where(cycle == j, cutoff[j], cut)
    for b in range(10):
        k = row + 8 * b
        mode = jnp.where(k > TOP, k - TOP, k)
        kept = (mode <= cut) & (k <= 2 * TOP)
        WT[8 * b : 8 * b + 8] = jnp.where(kept, jnp.where(k == 0, 1.0 / NT, 2.0 / NT), 0.0)

    zero = jnp.zeros((8, 128), jnp.float32)
    for q in range(4):
        for c in range(5):
            SI[q, c, 0:8] = zero
            SI[q, c, 40:48] = zero
    for c in range(5):
        for g in range(4):
            FA[0, c, 8 * g : 8 * g + 8] = zero
            FA[5, c, 8 * g : 8 * g + 8] = zero
    for e in range(8):
        SB[e, 32:40] = zero

    for c in loads[0]:
        c.wait()
    for l in range(1, LT):
        for c in loads[l]:
            c.start()
    small[2].start()
    small[3].start()

    def inner(q, _):
        for g in range(4):
            r = pl.ds(8 + 8 * g, 8)
            o = pl.ds(8 * g, 8)
            raw = [[ST[0, f, 4 * q + 1 + i, r] for i in range(4)] for f in range(5)]
            st = [pack(xs) for xs in raw]
            nx = []
            for xs in raw:
                got = pltpu.roll(xs[0], 127, 1)
                for i in range(1, 4):
                    got = jnp.where(lane >= 32 * i, pltpu.roll(xs[i], 32 * i - 1, 1), got)
                nx.append(got)
            level = pack([SP[0, 4 * q + i, o] for i in range(4)]).astype(jnp.float32) * (time_step * sponge_rate)
            density, mx, mr, ms, energy = st
            u, v, w, a, b, c, pressure, h = prims(st)
            a2, a3, s2, s3 = mr * u, ms * u, mr * w, c + pressure
            for k, x in enumerate((mx, a + pressure, a2, a3, h * u)):
                FA[q + 1, k, o] = x
            for k, x in enumerate((ms, a3, s2, s3, h * w)):
                SI[q, k, r] = x
            behind = [pltpu.roll(x, 1, 1) for x in (mr, a2, b + pressure, s2, h * v)]
            nu, nv, nw, na, nb, nc, npres, nh = prims(nx)
            ahead = (nx[2], nx[1] * nv, nb + npres, nx[3] * nv, nh * nv)
            for f in range(5):
                part = st[f] - level * (st[f] - PC[4 + f]) - (ahead[f] * PC[0] - behind[f] * PC[1])
                if f == 2:
                    part = part + PC[3] * s3
                if f == 3:
                    part = part - PC[3] * s2
                PI[q, f, o] = part
        return 0

    lax.fori_loop(0, 4, inner, 0)

    def hello(side, y):
        return pltpu.make_async_remote_copy(
            src_ref=HS.at[side, y], dst_ref=HR.at[az], send_sem=hs_send.at[side, y], recv_sem=hs_recv.at[az],
            device_id={"gx": up, "az": jnp.int32(4 * y)} if side == 0 else {"gx": down, "az": jnp.int32(4 * y + 3)},
        )

    for side in range(2):
        for f in range(5):
            xs = [FA[4 if side == 0 else 1, f, 8 * g : 8 * g + 8] for g in range(4)]
            if side == 0:
                got = pltpu.roll(xs[0], 32, 1)
                for g in range(1, 4):
                    x = pltpu.roll(xs[g], 32 * (g + 1), 1) if g < 3 else xs[g]
                    got = jnp.where(lane >= 32 * g, x, got)
            else:
                got = pack(xs)
            if f == 2:
                HS[side, 0, 16:24] = got
                HS[side, 1, 16:24] = got
            else:
                s = f if f < 2 else f - 3
                HS[side, f // 3, 8 * s : 8 * s + 8] = got

    PARTS = ((0, 40), (40, 48))

    def forth(part, e):
        at, size = PARTS[part]
        return pltpu.make_async_remote_copy(
            src_ref=SB.at[e, at : at + size], dst_ref=RB.at[az, at : at + size],
            send_sem=send1.at[part, e], recv_sem=recv1.at[part, az], device_id={"az": e},
        )

    def made(q, f):
        xs = []
        for g in range(4):
            o = pl.ds(8 * g, 8)
            own = FA[q + 1, f, o]
            above = pltpu.roll(jnp.where(lane < 32, FA[q + 2, f, o], own), 96, 1)
            below = pltpu.roll(jnp.where(lane >= 96, FA[q, f, o], own), 32, 1)
            swirl_diff = SI[q, f, pl.ds(9 + 8 * g, 8)] - SI[q, f, pl.ds(7 + 8 * g, 8)]
            xs.append(PI[q, f, o] - PC[9 + q] * (above - below) - PC[2] * swirl_diff)
        return xs

    def group_a(q, _):
        for f in range(5):
            first = -PC[2] * SI[q, f, 8:16]
            last = PC[2] * SI[q, f, 32:40]
            if f != 2:
                e = q if f < 2 else q + 4
                s = f if f < 2 else f - 3
                SB[e, 32 + 2 * s : 33 + 2 * s] = first[0:1]
                SB[e, 33 + 2 * s : 34 + 2 * s] = last[7:8]
                if s == 0:
                    xs = made(q, f)
                    for g in range(4):
                        SB[e, 8 * g : 8 * g + 8] = xs[g]
            else:
                low = lax.broadcasted_iota(jnp.int32, (1, 128), 1) < 64
                SB[q, 36:37] = jnp.where(low, last[7:8], pltpu.roll(first, 64, 1)[0:1])
                SB[q + 4, 36:37] = jnp.where(low, pltpu.roll(last, 64, 1)[7:8], first[0:1])
        return 0

    def group_b(q, _):
        for f in (1, 4):
            e = q if f < 2 else q + 4
            xs = made(q, f)
            for g in range(4):
                SB[e, 40 + 8 * g : 48 + 8 * g] = xs[g]
        xs = made(q, 2)
        half = lane < 64
        for g in range(2):
            SB[q, 72 + 8 * g : 80 + 8 * g] = jnp.where(half, xs[g], pltpu.roll(xs[g + 2], 64, 1))
            SB[q + 4, 72 + 8 * g : 80 + 8 * g] = jnp.where(half, pltpu.roll(xs[g], 64, 1), xs[g + 2])
        return 0

    def sent(part):
        at, size = PARTS[part]
        for k in range(1, 8):
            forth(part, lax.rem(az + k, n_az)).start()
        RB[az, at : at + size] = SB[az, at : at + size]

    lax.fori_loop(0, 4, group_a, 0)
    pl.semaphore_wait(barrier, greeted)
    sent(0)
    for side in range(2):

        @pl.when(sends_to[side])
        def _():
            for y in range(2):
                hello(side, y).start()

    lax.fori_loop(0, 4, group_b, 0)
    sent(1)
    for l in range(LT):
        for s in range(2):
            swirls[l][s].start()
    for s in range(2):

        @pl.when(direct[s])
        def _():
            for l in range(LT):
                axials[l][s].start()

    def leg(l, side):
        plane = 15 if side == 0 else 0
        return pltpu.make_async_remote_copy(
            src_ref=state.at[:, plane : plane + 1, :, lanes(l)], dst_ref=RL,
            send_sem=ax_send.at[l, side], recv_sem=rl_recv,
            device_id={"gx": jnp.int32((up_relay if side == 0 else down_relay)[l]), "az": partner},
        )

    def relay(l, side):
        slot = 0 if side == 0 else 17
        return pltpu.make_async_remote_copy(
            src_ref=RL, dst_ref=ST.at[l, :, slot : slot + 1, 8:40, :],
            send_sem=rl_send, recv_sem=ax_recv.at[l, side],
            device_id={"gx": jnp.int32(mid if side == 0 else mid - 1), "az": partner},
        )

    starts = (gx == mid - 1, gx == mid)
    for s in range(2):

        @pl.when(starts[s])
        def _():
            for l in range(LT):
                leg(l, s).start()

    SWIRL = (7, 2, 4, 5, 6)

    def axial_fluxes(l, p, r, st):
        density, mx, mr, ms, energy = st
        u, v, w, a, b, c, pressure, h = prims(st)
        FX[l, 0, p, r] = a + pressure
        a2 = mr * u
        FX[l, 1, p, r] = a2
        FX[l, 2, p, r] = ms * u
        FX[l, 3, p, r] = h * u
        return v, w, b, c, pressure, h, a2

    def swirl_fluxes(l, p, r, mr, ms, w, c, pressure, h):
        s2 = mr * w
        s3 = c + pressure
        FX[l, 4, p, r] = s2
        FX[l, 5, p, r] = s3
        FX[l, 6, p, r] = h * w
        FX[l, 7, p, r] = ms
        return s2, s3

    def block(p, g):
        r = pl.ds(8 + 8 * g, 8)
        states, radials, sources = [], [], []
        for l in range(LT):
            st = [ST[l, f, p, r] for f in range(5)]
            mr, ms = st[2], st[3]
            v, w, b, c, pressure, h, a2 = axial_fluxes(l, p, r, st)
            s2, s3 = swirl_fluxes(l, p, r, mr, ms, w, c, pressure, h)
            states.append(st)
            radials.append((mr, a2, b + pressure, s2, h * v))
            sources.append((s2, s3))
        fwd = [[pltpu.roll(x, 127, 1) for x in rs] for rs in radials]
        bwd = [[pltpu.roll(x, 1, 1) for x in rs] for rs in radials]
        for l in range(LT):
            level = SP[l, p - 1, pl.ds(8 * g, 8)].astype(jnp.float32) * (time_step * sponge_rate)
            for f in range(5):
                ahead, behind = fwd[l][f], bwd[l][f]
                if l + 1 < LT:
                    ahead = jnp.where(lane == 127, fwd[l + 1][f], ahead)
                if l > 0:
                    behind = jnp.where(lane == 0, bwd[l - 1][f], behind)
                x = states[l][f]
                part = x - level * (x - LC[4 + f, l]) - (ahead * LC[0, l] - behind * LC[1, l])
                if f == 2:
                    part = part + LC[3, l] * sources[l][1]
                if f == 3:
                    part = part - LC[3, l] * sources[l][0]
                PART[l, f, p - 1, pl.ds(8 * g, 8)] = part

    for l in range(1, LT):
        for c in loads[l]:
            c.wait()

    def outer(p, _):
        for g in range(4):
            block(p, g)
        return 0

    lax.fori_loop(1, N1, outer, 0)

    small[2].wait()
    small[3].wait()

    def arrived(part):
        at, size = PARTS[part]
        for k in range(1, 8):
            s = lax.rem(az + k, n_az)
            pltpu.make_async_remote_copy(
                src_ref=SB.at[s, at : at + size], dst_ref=RB.at[s, at : at + size],
                send_sem=send1.at[part, s], recv_sem=recv1.at[part, s], device_id={"az": s},
            ).wait_recv()

    def neighbours():
        for side in range(2):

            @pl.when(gets_from[side] & (first_x if side == 0 else last_x))
            def _():
                for d in range(8):
                    pltpu.make_async_remote_copy(
                        src_ref=HS.at[0, 0], dst_ref=HR.at[d], send_sem=hs_send.at[0, 0], recv_sem=hs_recv.at[d],
                        device_id={"gx": up},
                    ).wait_recv()

    def edges(part):
        for side in range(2):

            @pl.when(gets_from[side] & (first_x if side == 0 else last_x))
            def _():
                scale = (0.5 * time_step) * inv_dx[0] if side == 0 else (-0.5 * time_step) * inv_dx[PL_DEV - 1]
                for d in range(8):
                    for s in (0,) if part == 0 else (1, 2):
                        x = HR[d, 8 * s : 8 * s + 8] * scale
                        for g in range(4):
                            if s < 2:
                                to, base = 40 * s + 8 * g, 0 if side == 0 else 96
                            else:
                                to, base = 72 + 8 * (g % 2), 64 * (g // 2) + (0 if side == 0 else 32)
                            here = (lane >= base) & (lane < base + 32)
                            if s == 2:
                                here = here & (az == (0 if side == 0 else 7))
                            y = pltpu.roll(x, (base - 32 * g) % 128, 1) if (base - 32 * g) % 128 else x
                            RB[d, to : to + 8] += jnp.where(here, y, 0.0)

        low1 = lax.broadcasted_iota(jnp.int32, (1, 128), 1) < 64
        for d in range(8):
            prev, nxt = (d + 7) % 8, (d + 1) % 8
            s = part
            RB[d, 40 * s : 40 * s + 1] += RB[prev, 33 + 2 * s : 34 + 2 * s]
            RB[d, 40 * s + 31 : 40 * s + 32] += RB[nxt, 32 + 2 * s : 33 + 2 * s]
            if part == 1:
                RB[d, 72:73] += jnp.where(low1, RB[prev, 36:37], 0.0)
                RB[d, 87:88] += jnp.where(low1, 0.0, RB[nxt, 36:37])

    half16 = lax.broadcasted_iota(jnp.int32, (16, 128), 1) < 64
    BACKS = ((0, 32), (32, 48))

    def filtered(part):
        for s in (0,) if part == 0 else (1, 2):
            if s < 2:
                xs = [RB[d, 40 * s : 40 * s + 32] for d in range(8)]
            else:
                xs = []
                for d in range(8):
                    t = RB[d, 72:88]
                    xs += [t, pltpu.roll(t, 64, 1)]
            x = jnp.concatenate(xs, 0)
            high = x.astype(jnp.bfloat16)
            low = (x - high.astype(jnp.float32)).astype(jnp.bfloat16)
            both = jnp.dot(CC[...], high, preferred_element_type=jnp.float32)
            coef = both[0:80] + both[80:160] + jnp.dot(CC[0:80], low, preferred_element_type=jnp.float32)
            z = coef * WT[...]
            zh = z.astype(jnp.bfloat16)
            zl = (z - zh.astype(jnp.float32)).astype(jnp.bfloat16)
            y = jnp.dot(TT[...], jnp.concatenate([zh, zh, zl], 0), preferred_element_type=jnp.float32)
            for d in range(8):
                yd = y[32 * d : 32 * d + 32]
                if s < 2:
                    SB2[d, 32 * s : 32 * s + 32] = yd
                else:
                    SB2[d, 64:80] = jnp.where(half16, yd[0:16], pltpu.roll(yd[16:32], 64, 1))

    def back(part, d, src):
        at, size = BACKS[part]
        return pltpu.make_async_remote_copy(
            src_ref=SB2.at[d, at : at + size], dst_ref=R2.at[src, at : at + size],
            send_sem=send2.at[part, d], recv_sem=recv2.at[part, src], device_id={"az": d},
        )

    def returned(part):
        at, size = BACKS[part]
        for k in range(1, 8):
            back(part, lax.rem(az + k, n_az), az).start()
        R2[az, at : at + size] = SB2[az, at : at + size]

    arrived(0)
    neighbours()
    edges(0)
    filtered(0)
    returned(0)
    for l in range(LT):
        for s in range(2):

            @pl.when(gx == (up_relay if s == 0 else down_relay)[l])
            def _():
                leg(l, s).wait_recv()
                relay(l, s).start()

    lax.fori_loop(N1, 17, outer, 0)
    arrived(1)
    edges(1)
    filtered(1)
    returned(1)

    for s in range(2):
        for l in range(LT):
            swirls[l][s].wait_recv()

    def pads(p, _):
        for l in range(LT):
            for r0 in (0, 40):
                r = pl.ds(r0, 8)
                st = [ST[l, f, p, r] for f in range(5)]
                u, v, w, a, b, c, pressure, h = prims(st)
                FX[l, 2, p, r] = st[3] * u
                swirl_fluxes(l, p, r, st[2], st[3], w, c, pressure, h)
        return 0

    lax.fori_loop(1, 17, pads, 0)

    def finish(p, _):
        step = (0.5 * time_step) * inv_dx[p - 1]
        for l in range(LT):
            for f in range(5):
                for g in range(4):
                    r = pl.ds(8 + 8 * g, 8)
                    if f == 0:
                        above, below = ST[l, 1, p + 1, r], ST[l, 1, p - 1, r]
                    else:
                        above, below = FX[l, f - 1, p + 1, r], FX[l, f - 1, p - 1, r]
                    c = SWIRL[f]
                    turn = FX[l, c, p, pl.ds(9 + 8 * g, 8)] - FX[l, c, p, pl.ds(7 + 8 * g, 8)]
                    x = PART[l, f, p - 1, pl.ds(8 * g, 8)]
                    x = x - step * (above - below) - LC[2, l] * turn
                    out[f, p - 1, 8 * g : 8 * g + 8, l * 128 : (l + 1) * 128] = x
        return 0

    lax.fori_loop(2, 16, finish, 0)
    for s in range(2):
        p = 0 if s == 0 else 17

        @pl.when(gets_from[s])
        def _():
            for l in range(LT):
                axials[l][s].wait_recv()
                for g in range(4):
                    r = pl.ds(8 + 8 * g, 8)
                    axial_fluxes(l, p, r, [ST[l, f, p, r] for f in range(5)])

        @pl.when(jnp.logical_not(gets_from[s]))
        def _():
            for l in range(LT):
                for g in range(4):
                    r = pl.ds(8 + 8 * g, 8)
                    ST[l, 1, p, r] = zero
                    for k in range(4):
                        FX[l, k, p, r] = zero

        finish(1 if s == 0 else 16, 0)

    for s in range(2):
        for l in range(LT):
            swirls[l][s].wait_send()

        @pl.when(sends_to[s])
        def _():
            for l in range(LT):
                axials[l][s].wait_send()
            for y in range(2):
                hello(s, y).wait_send()

        for l in range(LT):

            @pl.when(gx == (up_relay if s == 0 else down_relay)[l])
            def _():
                relay(l, s).wait_send()

    for k in range(1, 8):
        e = lax.rem(az + k, n_az)
        for part in range(2):
            forth(part, e).wait_send()
            back(part, e, az).wait_send()
            back(part, e, e).wait_recv()


def write(partial, filtered, out, T0, sem, sem0):
    rest = pltpu.make_async_copy(
        partial.at[:, :, :, 128:NR], out.at[:, :, :, 128:NR], sem
    )
    rest.start()
    lane = lax.broadcasted_iota(jnp.int32, (8, 128), 1)

    def tile(q):
        return pltpu.make_async_copy(
            T0.at[:, pl.ds(4 * q, 4)], out.at[:, pl.ds(4 * q, 4), :, 0:128], sem0.at[q]
        )

    def merge(q, _):
        for i in range(4):
            p = 4 * q + i
            for f in range(5):
                for g in range(4):
                    if f != 2:
                        e = q if f < 2 else q + 4
                        s = f if f < 2 else f - 3
                        x = filtered[e, 32 * s + 8 * g : 32 * s + 8 * g + 8]
                        base = 32 * i
                    else:
                        e = q if i < 2 else q + 4
                        x = filtered[e, 64 + 8 * (g % 2) : 72 + 8 * (g % 2)]
                        base = 32 * (i % 2) + 64 * (g // 2)
                    if base:
                        x = pltpu.roll(x, 128 - base, 1)
                    old = partial[f, p, 8 * g : 8 * g + 8, 0:128]
                    T0[f, p, 8 * g : 8 * g + 8] = jnp.where(lane < CYCLE, x, old)
        tile(q).start()
        return 0

    lax.fori_loop(0, 4, merge, 0)
    for q in range(4):
        tile(q).wait()
    rest.wait()


def solution(mesh):
    fwd, inv = tables()

    def body(state, sponge_level, inv_dx, inv_dr, target, cutoff):
        f32 = jnp.float32
        hbm = pl.BlockSpec(memory_space=pltpu.HBM)
        vmem = pl.BlockSpec(memory_space=pltpu.VMEM)
        dma = pltpu.SemaphoreType.DMA
        args = (state, sponge_level, inv_dr.reshape(1, NR), target, jnp.asarray(fwd), jnp.asarray(inv), inv_dx, cutoff)
        args = [pltpu.with_memory_space_constraint(x, pltpu.HBM) for x in args]
        partial, filtered = pl.pallas_call(
            kernel,
            out_shape=(pltpu.VMEM(state.shape, f32), pltpu.VMEM((8, BACK, 128), f32)),
            in_specs=[hbm] * 8,
            out_specs=(vmem, vmem),
            scratch_shapes=[
                pltpu.VMEM((LT, 5, 18, 48, 128), f32),
                pltpu.VMEM((LT, 8, 18, 48, 128), f32),
                pltpu.VMEM((LT, 5, 16, 32, 128), f32),
                pltpu.VMEM((LT, 16, 32, 128), jnp.int32),
                pltpu.VMEM((5, NR), f32),
                pltpu.VMEM((1, NR), f32),
                pltpu.VMEM(fwd.shape, jnp.bfloat16),
                pltpu.VMEM(inv.shape, jnp.bfloat16),
                pltpu.VMEM((9, LT, 8, 128), f32),
                pltpu.VMEM((13, 8, 128), f32),
                pltpu.VMEM((4, 5, 32, 128), f32),
                pltpu.VMEM((6, 5, 32, 128), f32),
                pltpu.VMEM((4, 5, 48, 128), f32),
                pltpu.VMEM((8, ROWS, 128), f32),
                pltpu.VMEM((8, ROWS, 128), f32),
                pltpu.VMEM((8, BACK, 128), f32),
                pltpu.VMEM((2, 2, 24, 128), f32),
                pltpu.VMEM((8, 24, 128), f32),
                pltpu.VMEM((5, 1, CELLS, 128), f32),
                pltpu.VMEM((80, 128), f32),
                pltpu.SMEM((PL_DEV,), f32),
                pltpu.SMEM((CYCLE,), jnp.int32),
                dma((2 * LT,)),
                dma((6,)),
                dma((LT, 2)),
                dma((LT, 2)),
                dma((LT, 2)),
                dma((LT, 2)),
                dma((2, 8)),
                dma((2, 8)),
                dma((2, 8)),
                dma((2, 8)),
                dma((2, 2)),
                dma((8,)),
                dma(()),
                dma(()),
            ],
            compiler_params=pltpu.CompilerParams(collective_id=0, has_side_effects=True, vmem_limit_bytes=48 << 20),
        )(*args)
        partial, filtered = (pltpu.with_memory_space_constraint(x, pltpu.VMEM) for x in (partial, filtered))
        return pl.pallas_call(
            write,
            out_shape=jax.ShapeDtypeStruct(state.shape, f32),
            in_specs=[vmem, vmem],
            out_specs=hbm,
            scratch_shapes=[pltpu.VMEM((5, PL_DEV, CELLS, 128), f32), dma(()), dma((4,))],
            compiler_params=pltpu.CompilerParams(vmem_limit_bytes=4 << 20),
        )(partial, filtered)

    return jax.shard_map(
        body,
        mesh=mesh,
        in_specs=(P(None, "gx", "az", None), P("gx", "az", None), P("gx"), P(), P(), P()),
        out_specs=P(None, "gx", "az", None),
        check_vma=False,
    )
```

```python
import jax
import jax.numpy as jnp
import numpy as np
from jax import lax
from jax.experimental import pallas as pl
from jax.experimental.pallas import tpu as pltpu
from jax.sharding import PartitionSpec as P

NT = 256
CYCLE = 32
NR = 512
PL_DEV = 16
CELLS = 32
TOP = 32
LT = NR // 128

time_step = 0.02
sponge_rate = 4.0

ROWS = 88
BACK = 80
N1 = 14
ORDER = (1, 2, 3, 4, 5, 6, 7)
SPREAD = (1, 1, 1, 1)


def tables():
    cell = np.arange(NT)
    cos = np.cos(2 * np.pi * ((np.arange(TOP + 1)[:, None] * cell[None]) % NT) / NT)
    sin = np.sin(2 * np.pi * ((np.arange(1, TOP + 1)[:, None] * cell[None]) % NT) / NT)
    whole = np.zeros((80, NT), np.float32)
    whole[: TOP + 1] = cos
    whole[TOP + 1 : 2 * TOP + 1] = sin
    high = whole.astype(jnp.bfloat16)
    low = (whole - high.astype(np.float32)).astype(jnp.bfloat16)
    fwd = np.concatenate([high, low], 0)
    inv = np.concatenate([high.T, low.T, high.T], 1)
    return fwd, inv


def prims(st):
    density, mx, mr, ms, energy = st
    inv = 1.0 / density
    u = mx * inv
    v = mr * inv
    w = ms * inv
    a = mx * u
    b = mr * v
    c = ms * w
    pressure = 0.4 * (energy - 0.5 * (a + b + c))
    return u, v, w, a, b, c, pressure, energy + pressure


def kernel(
    state, sponge, inv_dr, target, fwd_t, inv_t, inv_dx_in, cutoff_in, out, R2,
    ST, FX, PART, SP, TG, IDR, CC, TT, LC, PC, PI, FA, SI, SB, RB, SB2, HS, HR, RL, WT, inv_dx, cutoff,
    load_sem, small_sem, ax_send, ax_recv, sw_send, sw_recv, send1, recv1, send2, recv2, hs_send, hs_recv,
    rl_send, rl_recv,
):
    gx = lax.axis_index("gx")
    az = lax.axis_index("az")
    n_gx = lax.axis_size("gx")
    n_az = lax.axis_size("az")
    has_up, has_down = gx < n_gx - 1, gx > 0
    up, down = lax.rem(gx + 1, n_gx), lax.rem(gx + n_gx - 1, n_gx)
    east, west = lax.rem(az + 1, n_az), lax.rem(az + n_az - 1, n_az)
    partner = lax.rem(az + 4, n_az)
    mid = n_gx // 2
    up_relay = [1 + 2 * l for l in range(LT)]
    down_relay = [n_gx - 1 - 2 * l for l in range(LT)]
    first_x, last_x = lax.rem(az, 4) == 0, lax.rem(az, 4) == 3

    def lanes(l):
        return pl.ds(l * 128, 128)

    loads = []
    for l in range(LT):
        loads.append(
            (
                pltpu.make_async_copy(
                    state.at[:, :, :, lanes(l)],
                    ST.at[l, :, 1:17, 8:40, :],
                    load_sem.at[2 * l],
                ),
                pltpu.make_async_copy(
                    sponge.at[:, :, lanes(l)], SP.at[l], load_sem.at[2 * l + 1]
                ),
            )
        )
    small = [
        pltpu.make_async_copy(inv_dr, IDR, small_sem.at[0]),
        pltpu.make_async_copy(target, TG, small_sem.at[1]),
        pltpu.make_async_copy(fwd_t, CC, small_sem.at[2]),
        pltpu.make_async_copy(inv_t, TT, small_sem.at[3]),
        pltpu.make_async_copy(inv_dx_in, inv_dx, small_sem.at[4]),
        pltpu.make_async_copy(cutoff_in, cutoff, small_sem.at[5]),
    ]
    for k in (0, 1, 4, 5):
        small[k].start()
    for c in loads[0]:
        c.start()
    barrier = pltpu.get_barrier_semaphore()
    for k in range(1, n_az):
        pl.semaphore_signal(barrier, inc=1, device_id={"az": lax.rem(az + k, n_az)})
    for there, g, holds in ((has_down, down, first_x), (has_up, up, last_x)):

        @pl.when(there)
        def _():
            pl.semaphore_signal(barrier, inc=1, device_id={"gx": g})

        @pl.when(there & holds)
        def _():
            for d in range(8):
                pl.semaphore_signal(barrier, inc=1, device_id={"gx": g, "az": jnp.int32(d)})

    relays = 0
    for l in range(LT):
        for g, to in (
            (up_relay[l], mid - 1), (mid, up_relay[l]), (down_relay[l], mid), (mid - 1, down_relay[l])
        ):
            if g != to:

                @pl.when(gx == g)
                def _():
                    pl.semaphore_signal(barrier, inc=1, device_id={"gx": jnp.int32(to), "az": partner})

                relays = relays + (gx == to).astype(jnp.int32)
    greeted = n_az - 1 + 3 * has_up.astype(jnp.int32) + 3 * has_down.astype(jnp.int32) + relays


    def axial(l, side):
        plane = 15 if side == 0 else 0
        slot = 0 if side == 0 else 17
        return pltpu.make_async_remote_copy(
            src_ref=state.at[:, plane : plane + 1, :, lanes(l)],
            dst_ref=ST.at[l, :, slot : slot + 1, 8:40, :],
            send_sem=ax_send.at[l, side],
            recv_sem=ax_recv.at[l, side],
            device_id={"gx": up if side == 0 else down},
        )

    def swirl(l, side):
        row = 31 if side == 0 else 0
        slot = 7 if side == 0 else 40
        return pltpu.make_async_remote_copy(
            src_ref=state.at[:, :, row : row + 1, lanes(l)],
            dst_ref=ST.at[l, :, 1:17, slot : slot + 1, :],
            send_sem=sw_send.at[l, side],
            recv_sem=sw_recv.at[l, side],
            device_id={"az": east if side == 0 else west},
        )

    axials = [[axial(l, s) for s in range(2)] for l in range(LT)]
    swirls = [[swirl(l, s) for s in range(2)] for l in range(LT)]
    sends_to = (has_up, has_down)
    direct = (has_up & (gx != mid - 1), has_down & (gx != mid))
    gets_from = (has_down, has_up)

    lane = lax.broadcasted_iota(jnp.int32, (8, 128), 1)
    row = lax.broadcasted_iota(jnp.int32, (8, 128), 0)
    cycle = lane & (CYCLE - 1)

    def pack(xs):
        got = xs[0]
        for i in range(1, 4):
            got = jnp.where(lane >= 32 * i, pltpu.roll(xs[i], 32 * i, 1), got)
        return got

    for k in (0, 1, 4, 5):
        small[k].wait()

    def coefficients(j, spacing):
        jf = j.astype(jnp.float32)
        after = 1.0 + 4.0 * (jf + 1.0) / NR
        before = 1.0 + 4.0 * (jf - 1.0) / NR
        inv_r = 1.0 / (1.0 + 4.0 * jf / NR)
        rr = (0.5 * time_step) * spacing * inv_r
        return (
            jnp.where(j == NR - 1, 0.0, rr * after),
            jnp.where(j == 0, 0.0, rr * before),
            (time_step * NT / (4.0 * np.pi)) * inv_r,
            time_step * inv_r,
        )

    def wide(ref, f, l):
        return jnp.broadcast_to(ref[f : f + 1, l * 128 : (l + 1) * 128], (8, 128))

    for k, x in enumerate(coefficients(cycle, pack([wide(IDR, 0, 0)] * 4))):
        PC[k] = x
    for f in range(5):
        PC[4 + f] = pack([wide(TG, f, 0)] * 4)
    for q in range(4):
        x = jnp.zeros((8, 128), jnp.float32)
        for i in range(4):
            x = jnp.where(lane >= 32 * i, (0.5 * time_step) * inv_dx[4 * q + i], x)
        PC[9 + q] = x
    for l in range(LT):
        for k, x in enumerate(coefficients(lane + l * 128, wide(IDR, 0, l))):
            LC[k, l] = x
        for f in range(5):
            LC[4 + f, l] = wide(TG, f, l)

    cut = jnp.zeros((8, 128), jnp.int32)
    for j in range(CYCLE):
        cut = jnp.where(cycle == j, cutoff[j], cut)
    for b in range(10):
        k = row + 8 * b
        mode = jnp.where(k > TOP, k - TOP, k)
        kept = (mode <= cut) & (k <= 2 * TOP)
        WT[8 * b : 8 * b + 8] = jnp.where(kept, jnp.where(k == 0, 1.0 / NT, 2.0 / NT), 0.0)

    zero = jnp.zeros((8, 128), jnp.float32)
    for q in range(4):
        for c in range(5):
            SI[q, c, 0:8] = zero
            SI[q, c, 40:48] = zero
    for c in range(5):
        for g in range(4):
            FA[0, c, 8 * g : 8 * g + 8] = zero
            FA[5, c, 8 * g : 8 * g + 8] = zero
    for e in range(8):
        SB[e, 32:40] = zero

    for c in loads[0]:
        c.wait()
    for l in range(1, LT):
        for c in loads[l]:
            c.start()
    small[2].start()
    small[3].start()

    def inner(q, _):
        for g in range(4):
            r = pl.ds(8 + 8 * g, 8)
            o = pl.ds(8 * g, 8)
            raw = [[ST[0, f, 4 * q + 1 + i, r] for i in range(4)] for f in range(5)]
            st = [pack(xs) for xs in raw]
            nx = []
            for xs in raw:
                got = pltpu.roll(xs[0], 127, 1)
                for i in range(1, 4):
                    got = jnp.where(lane >= 32 * i, pltpu.roll(xs[i], 32 * i - 1, 1), got)
                nx.append(got)
            level = pack([SP[0, 4 * q + i, o] for i in range(4)]).astype(jnp.float32) * (time_step * sponge_rate)
            density, mx, mr, ms, energy = st
            u, v, w, a, b, c, pressure, h = prims(st)
            a2, a3, s2, s3 = mr * u, ms * u, mr * w, c + pressure
            for k, x in enumerate((mx, a + pressure, a2, a3, h * u)):
                FA[q + 1, k, o] = x
            for k, x in enumerate((ms, a3, s2, s3, h * w)):
                SI[q, k, r] = x
            behind = [pltpu.roll(x, 1, 1) for x in (mr, a2, b + pressure, s2, h * v)]
            nu, nv, nw, na, nb, nc, npres, nh = prims(nx)
            ahead = (nx[2], nx[1] * nv, nb + npres, nx[3] * nv, nh * nv)
            for f in range(5):
                part = st[f] - level * (st[f] - PC[4 + f]) - (ahead[f] * PC[0] - behind[f] * PC[1])
                if f == 2:
                    part = part + PC[3] * s3
                if f == 3:
                    part = part - PC[3] * s2
                PI[q, f, o] = part
        return 0

    def send_swirl(when):
        for l in range(LT):
            if SPREAD[l] == when:
                for s in range(2):
                    swirls[l][s].start()

    lax.fori_loop(0, 4, inner, 0)

    def hello(side, y):
        return pltpu.make_async_remote_copy(
            src_ref=HS.at[side, y], dst_ref=HR.at[az], send_sem=hs_send.at[side, y], recv_sem=hs_recv.at[az],
            device_id={"gx": up, "az": jnp.int32(4 * y)} if side == 0 else {"gx": down, "az": jnp.int32(4 * y + 3)},
        )

    for side in range(2):
        for f in range(5):
            xs = [FA[4 if side == 0 else 1, f, 8 * g : 8 * g + 8] for g in range(4)]
            if side == 0:
                got = pltpu.roll(xs[0], 32, 1)
                for g in range(1, 4):
                    x = pltpu.roll(xs[g], 32 * (g + 1), 1) if g < 3 else xs[g]
                    got = jnp.where(lane >= 32 * g, x, got)
            else:
                got = pack(xs)
            if f == 2:
                HS[side, 0, 16:24] = got
                HS[side, 1, 16:24] = got
            else:
                s = f if f < 2 else f - 3
                HS[side, f // 3, 8 * s : 8 * s + 8] = got

    def leg(l, side):
        plane = 15 if side == 0 else 0
        return pltpu.make_async_remote_copy(
            src_ref=state.at[:, plane : plane + 1, :, lanes(l)], dst_ref=RL,
            send_sem=ax_send.at[l, side], recv_sem=rl_recv,
            device_id={"gx": jnp.int32((up_relay if side == 0 else down_relay)[l]), "az": partner},
        )

    def relay(l, side):
        slot = 0 if side == 0 else 17
        return pltpu.make_async_remote_copy(
            src_ref=RL, dst_ref=ST.at[l, :, slot : slot + 1, 8:40, :],
            send_sem=rl_send, recv_sem=ax_recv.at[l, side],
            device_id={"gx": jnp.int32(mid if side == 0 else mid - 1), "az": partner},
        )

    PARTS = ((0, 40), (40, 48))

    def forth(part, e):
        at, size = PARTS[part]
        return pltpu.make_async_remote_copy(
            src_ref=SB.at[e, at : at + size], dst_ref=RB.at[az, at : at + size],
            send_sem=send1.at[part, e], recv_sem=recv1.at[part, az], device_id={"az": e},
        )

    def made(q, f):
        xs = []
        for g in range(4):
            o = pl.ds(8 * g, 8)
            own = FA[q + 1, f, o]
            above = pltpu.roll(jnp.where(lane < 32, FA[q + 2, f, o], own), 96, 1)
            below = pltpu.roll(jnp.where(lane >= 96, FA[q, f, o], own), 32, 1)
            swirl_diff = SI[q, f, pl.ds(9 + 8 * g, 8)] - SI[q, f, pl.ds(7 + 8 * g, 8)]
            xs.append(PI[q, f, o] - PC[9 + q] * (above - below) - PC[2] * swirl_diff)
        return xs

    def group_a(q, _):
        for f in range(5):
            first = -PC[2] * SI[q, f, 8:16]
            last = PC[2] * SI[q, f, 32:40]
            if f != 2:
                e = q if f < 2 else q + 4
                s = f if f < 2 else f - 3
                SB[e, 32 + 2 * s : 33 + 2 * s] = first[0:1]
                SB[e, 33 + 2 * s : 34 + 2 * s] = last[7:8]
                if s == 0:
                    xs = made(q, f)
                    for g in range(4):
                        SB[e, 8 * g : 8 * g + 8] = xs[g]
            else:
                low = lax.broadcasted_iota(jnp.int32, (1, 128), 1) < 64
                SB[q, 36:37] = jnp.where(low, last[7:8], pltpu.roll(first, 64, 1)[0:1])
                SB[q + 4, 36:37] = jnp.where(low, pltpu.roll(last, 64, 1)[7:8], first[0:1])
        return 0

    def group_b(q, _):
        for f in (1, 4):
            e = q if f < 2 else q + 4
            xs = made(q, f)
            for g in range(4):
                SB[e, 40 + 8 * g : 48 + 8 * g] = xs[g]
        xs = made(q, 2)
        half = lane < 64
        for g in range(2):
            SB[q, 72 + 8 * g : 80 + 8 * g] = jnp.where(half, xs[g], pltpu.roll(xs[g + 2], 64, 1))
            SB[q + 4, 72 + 8 * g : 80 + 8 * g] = jnp.where(half, pltpu.roll(xs[g], 64, 1), xs[g + 2])
        return 0

    def sent(part):
        at, size = PARTS[part]
        for k in ORDER:
            forth(part, lax.rem(az + k, n_az)).start()
        RB[az, at : at + size] = SB[az, at : at + size]

    lax.fori_loop(0, 4, group_a, 0)
    pl.semaphore_wait(barrier, greeted)
    for side in range(2):

        @pl.when(sends_to[side])
        def _():
            for y in range(2):
                hello(side, y).start()

    for s in range(2):

        @pl.when(gx == (mid - 1, mid)[s])
        def _():
            for l in range(LT):
                leg(l, s).start()

    sent(0)
    lax.fori_loop(0, 4, group_b, 0)
    sent(1)
    send_swirl(1)
    for s in range(2):

        @pl.when(direct[s])
        def _():
            for l in range(LT):
                axials[l][s].start()

    SWIRL = (7, 2, 4, 5, 6)

    def axial_fluxes(l, p, r, st):
        density, mx, mr, ms, energy = st
        u, v, w, a, b, c, pressure, h = prims(st)
        FX[l, 0, p, r] = a + pressure
        a2 = mr * u
        FX[l, 1, p, r] = a2
        FX[l, 2, p, r] = ms * u
        FX[l, 3, p, r] = h * u
        return v, w, b, c, pressure, h, a2

    def swirl_fluxes(l, p, r, mr, ms, w, c, pressure, h):
        s2 = mr * w
        s3 = c + pressure
        FX[l, 4, p, r] = s2
        FX[l, 5, p, r] = s3
        FX[l, 6, p, r] = h * w
        FX[l, 7, p, r] = ms
        return s2, s3

    def block(p, g):
        r = pl.ds(8 + 8 * g, 8)
        states, radials, sources = [], [], []
        for l in range(LT):
            st = [ST[l, f, p, r] for f in range(5)]
            mr, ms = st[2], st[3]
            v, w, b, c, pressure, h, a2 = axial_fluxes(l, p, r, st)
            s2, s3 = swirl_fluxes(l, p, r, mr, ms, w, c, pressure, h)
            states.append(st)
            radials.append((mr, a2, b + pressure, s2, h * v))
            sources.append((s2, s3))
        fwd = [[pltpu.roll(x, 127, 1) for x in rs] for rs in radials]
        bwd = [[pltpu.roll(x, 1, 1) for x in rs] for rs in radials]
        for l in range(LT):
            level = SP[l, p - 1, pl.ds(8 * g, 8)].astype(jnp.float32) * (time_step * sponge_rate)
            for f in range(5):
                ahead, behind = fwd[l][f], bwd[l][f]
                if l + 1 < LT:
                    ahead = jnp.where(lane == 127, fwd[l + 1][f], ahead)
                if l > 0:
                    behind = jnp.where(lane == 0, bwd[l - 1][f], behind)
                x = states[l][f]
                part = x - level * (x - LC[4 + f, l]) - (ahead * LC[0, l] - behind * LC[1, l])
                if f == 2:
                    part = part + LC[3, l] * sources[l][1]
                if f == 3:
                    part = part - LC[3, l] * sources[l][0]
                PART[l, f, p - 1, pl.ds(8 * g, 8)] = part

    for l in range(1, LT):
        for c in loads[l]:
            c.wait()

    def outer(p, _):
        for g in range(4):
            block(p, g)
        return 0

    lax.fori_loop(1, N1, outer, 0)

    small[2].wait()
    small[3].wait()

    def arrived(part):
        at, size = PARTS[part]
        for k in range(1, 8):
            s = lax.rem(az + k, n_az)
            pltpu.make_async_remote_copy(
                src_ref=SB.at[s, at : at + size], dst_ref=RB.at[s, at : at + size],
                send_sem=send1.at[part, s], recv_sem=recv1.at[part, s], device_id={"az": s},
            ).wait_recv()

    def neighbours():
        for side in range(2):

            @pl.when(gets_from[side] & (first_x if side == 0 else last_x))
            def _():
                for d in range(8):
                    pltpu.make_async_remote_copy(
                        src_ref=HS.at[0, 0], dst_ref=HR.at[d], send_sem=hs_send.at[0, 0], recv_sem=hs_recv.at[d],
                        device_id={"gx": up},
                    ).wait_recv()

    def edges(part):
        for side in range(2):

            @pl.when(gets_from[side] & (first_x if side == 0 else last_x))
            def _():
                scale = (0.5 * time_step) * inv_dx[0] if side == 0 else (-0.5 * time_step) * inv_dx[PL_DEV - 1]
                for d in range(8):
                    for s in (0,) if part == 0 else (1, 2):
                        x = HR[d, 8 * s : 8 * s + 8] * scale
                        for g in range(4):
                            if s < 2:
                                to, base = 40 * s + 8 * g, 0 if side == 0 else 96
                            else:
                                to, base = 72 + 8 * (g % 2), 64 * (g // 2) + (0 if side == 0 else 32)
                            here = (lane >= base) & (lane < base + 32)
                            if s == 2:
                                here = here & (az == (0 if side == 0 else 7))
                            y = pltpu.roll(x, (base - 32 * g) % 128, 1) if (base - 32 * g) % 128 else x
                            RB[d, to : to + 8] += jnp.where(here, y, 0.0)

        low1 = lax.broadcasted_iota(jnp.int32, (1, 128), 1) < 64
        for d in range(8):
            prev, nxt = (d + 7) % 8, (d + 1) % 8
            s = part
            RB[d, 40 * s : 40 * s + 1] += RB[prev, 33 + 2 * s : 34 + 2 * s]
            RB[d, 40 * s + 31 : 40 * s + 32] += RB[nxt, 32 + 2 * s : 33 + 2 * s]
            if part == 1:
                RB[d, 72:73] += jnp.where(low1, RB[prev, 36:37], 0.0)
                RB[d, 87:88] += jnp.where(low1, 0.0, RB[nxt, 36:37])

    half16 = lax.broadcasted_iota(jnp.int32, (16, 128), 1) < 64
    BACKS = ((0, 32), (32, 48))

    def filtered(part):
        for s in (0,) if part == 0 else (1, 2):
            if s < 2:
                xs = [RB[d, 40 * s : 40 * s + 32] for d in range(8)]
            else:
                xs = []
                for d in range(8):
                    t = RB[d, 72:88]
                    xs += [t, pltpu.roll(t, 64, 1)]
            x = jnp.concatenate(xs, 0)
            high = x.astype(jnp.bfloat16)
            low = (x - high.astype(jnp.float32)).astype(jnp.bfloat16)
            both = jnp.dot(CC[...], high, preferred_element_type=jnp.float32)
            coef = both[0:80] + both[80:160] + jnp.dot(CC[0:80], low, preferred_element_type=jnp.float32)
            z = coef * WT[...]
            zh = z.astype(jnp.bfloat16)
            zl = (z - zh.astype(jnp.float32)).astype(jnp.bfloat16)
            y = jnp.dot(TT[...], jnp.concatenate([zh, zh, zl], 0), preferred_element_type=jnp.float32)
            for d in range(8):
                yd = y[32 * d : 32 * d + 32]
                if s < 2:
                    SB2[d, 32 * s : 32 * s + 32] = yd
                else:
                    SB2[d, 64:80] = jnp.where(half16, yd[0:16], pltpu.roll(yd[16:32], 64, 1))

    def back(part, d, src):
        at, size = BACKS[part]
        return pltpu.make_async_remote_copy(
            src_ref=SB2.at[d, at : at + size], dst_ref=R2.at[src, at : at + size],
            send_sem=send2.at[part, d], recv_sem=recv2.at[part, src], device_id={"az": d},
        )

    def returned(part):
        at, size = BACKS[part]
        for k in ORDER:
            back(part, lax.rem(az + k, n_az), az).start()
        R2[az, at : at + size] = SB2[az, at : at + size]

    arrived(0)
    neighbours()
    edges(0)
    filtered(0)
    returned(0)
    send_swirl(2)
    lax.fori_loop(N1, 17, outer, 0)
    arrived(1)
    edges(1)
    filtered(1)
    returned(1)
    for l in range(LT):
        for s in range(2):

            @pl.when(gx == (up_relay if s == 0 else down_relay)[l])
            def _():
                leg(l, s).wait_recv()
                relay(l, s).start()


    def finish(l, p):
        step = (0.5 * time_step) * inv_dx[p - 1]
        for r0 in (0, 40):
            r = pl.ds(r0, 8)
            st = [ST[l, f, p, r] for f in range(5)]
            u, v, w, a, b, c, pressure, h = prims(st)
            FX[l, 2, p, r] = st[3] * u
            swirl_fluxes(l, p, r, st[2], st[3], w, c, pressure, h)
        for f in range(5):
            for g in range(4):
                r = pl.ds(8 + 8 * g, 8)
                if f == 0:
                    above, below = ST[l, 1, p + 1, r], ST[l, 1, p - 1, r]
                else:
                    above, below = FX[l, f - 1, p + 1, r], FX[l, f - 1, p - 1, r]
                c = SWIRL[f]
                turn = FX[l, c, p, pl.ds(9 + 8 * g, 8)] - FX[l, c, p, pl.ds(7 + 8 * g, 8)]
                x = PART[l, f, p - 1, pl.ds(8 * g, 8)]
                x = x - step * (above - below) - LC[2, l] * turn
                out[f, p - 1, 8 * g : 8 * g + 8, l * 128 : (l + 1) * 128] = x

    for l in range(LT):
        for s in range(2):
            swirls[l][s].wait_recv()

        def planes(i, _, l=l):
            for k in range(2):
                finish(l, 2 * i + k)
            return 0

        lax.fori_loop(1, 8, planes, 0)

    for s in range(2):
        p = 0 if s == 0 else 17

        @pl.when(gets_from[s])
        def _():
            for l in range(LT):
                axials[l][s].wait_recv()
                for g in range(4):
                    r = pl.ds(8 + 8 * g, 8)
                    axial_fluxes(l, p, r, [ST[l, f, p, r] for f in range(5)])

        @pl.when(jnp.logical_not(gets_from[s]))
        def _():
            for l in range(LT):
                for g in range(4):
                    r = pl.ds(8 + 8 * g, 8)
                    ST[l, 1, p, r] = zero
                    for k in range(4):
                        FX[l, k, p, r] = zero

        for l in range(LT):
            finish(l, 1 if s == 0 else 16)

    for s in range(2):
        for l in range(LT):
            swirls[l][s].wait_send()

        @pl.when(sends_to[s])
        def _():
            for l in range(LT):
                axials[l][s].wait_send()
            for y in range(2):
                hello(s, y).wait_send()

        for l in range(LT):

            @pl.when(gx == (up_relay if s == 0 else down_relay)[l])
            def _():
                relay(l, s).wait_send()

    for k in range(1, 8):
        e = lax.rem(az + k, n_az)
        for part in range(2):
            forth(part, e).wait_send()
            back(part, e, az).wait_send()
            back(part, e, e).wait_recv()


def write(partial, filtered, out, T0, sem, sem0):
    rests = [
        pltpu.make_async_copy(
            partial.at[f, :, :, 128:NR], out.at[f, :, :, 128:NR], sem.at[f]
        )
        for f in range(5)
    ]
    for rest in rests:
        rest.start()
    lane = lax.broadcasted_iota(jnp.int32, (8, 128), 1)

    def tile(q):
        return pltpu.make_async_copy(
            T0.at[:, pl.ds(4 * q, 4)], out.at[:, pl.ds(4 * q, 4), :, 0:128], sem0.at[q]
        )

    def merge(q, _):
        for i in range(4):
            p = 4 * q + i
            for f in range(5):
                for g in range(4):
                    if f != 2:
                        e = q if f < 2 else q + 4
                        s = f if f < 2 else f - 3
                        x = filtered[e, 32 * s + 8 * g : 32 * s + 8 * g + 8]
                        base = 32 * i
                    else:
                        e = q if i < 2 else q + 4
                        x = filtered[e, 64 + 8 * (g % 2) : 72 + 8 * (g % 2)]
                        base = 32 * (i % 2) + 64 * (g // 2)
                    if base:
                        x = pltpu.roll(x, 128 - base, 1)
                    old = partial[f, p, 8 * g : 8 * g + 8, 0:128]
                    T0[f, p, 8 * g : 8 * g + 8] = jnp.where(lane < CYCLE, x, old)
        tile(q).start()
        return 0

    lax.fori_loop(0, 4, merge, 0)
    for q in range(4):
        tile(q).wait()
    for rest in rests:
        rest.wait()


def solution(mesh):
    fwd, inv = tables()

    def body(state, sponge_level, inv_dx, inv_dr, target, cutoff):
        f32 = jnp.float32
        hbm = pl.BlockSpec(memory_space=pltpu.HBM)
        vmem = pl.BlockSpec(memory_space=pltpu.VMEM)
        dma = pltpu.SemaphoreType.DMA
        args = (state, sponge_level, inv_dr.reshape(1, NR), target, jnp.asarray(fwd), jnp.asarray(inv), inv_dx, cutoff)
        args = [pltpu.with_memory_space_constraint(x, pltpu.HBM) for x in args]
        partial, filtered = pl.pallas_call(
            kernel,
            out_shape=(pltpu.VMEM(state.shape, f32), pltpu.VMEM((8, BACK, 128), f32)),
            in_specs=[hbm] * 8,
            out_specs=(vmem, vmem),
            scratch_shapes=[
                pltpu.VMEM((LT, 5, 18, 48, 128), f32),
                pltpu.VMEM((LT, 8, 18, 48, 128), f32),
                pltpu.VMEM((LT, 5, 16, 32, 128), f32),
                pltpu.VMEM((LT, 16, 32, 128), jnp.int32),
                pltpu.VMEM((5, NR), f32),
                pltpu.VMEM((1, NR), f32),
                pltpu.VMEM(fwd.shape, jnp.bfloat16),
                pltpu.VMEM(inv.shape, jnp.bfloat16),
                pltpu.VMEM((9, LT, 8, 128), f32),
                pltpu.VMEM((13, 8, 128), f32),
                pltpu.VMEM((4, 5, 32, 128), f32),
                pltpu.VMEM((6, 5, 32, 128), f32),
                pltpu.VMEM((4, 5, 48, 128), f32),
                pltpu.VMEM((8, ROWS, 128), f32),
                pltpu.VMEM((8, ROWS, 128), f32),
                pltpu.VMEM((8, BACK, 128), f32),
                pltpu.VMEM((2, 2, 24, 128), f32),
                pltpu.VMEM((8, 24, 128), f32),
                pltpu.VMEM((5, 1, CELLS, 128), f32),
                pltpu.VMEM((80, 128), f32),
                pltpu.SMEM((PL_DEV,), f32),
                pltpu.SMEM((CYCLE,), jnp.int32),
                dma((2 * LT,)),
                dma((6,)),
                dma((LT, 2)),
                dma((LT, 2)),
                dma((LT, 2)),
                dma((LT, 2)),
                dma((2, 8)),
                dma((2, 8)),
                dma((2, 8)),
                dma((2, 8)),
                dma((2, 2)),
                dma((8,)),
                dma(()),
                dma(()),
            ],
            compiler_params=pltpu.CompilerParams(collective_id=0, has_side_effects=True, vmem_limit_bytes=48 << 20),
        )(*args)
        partial, filtered = (pltpu.with_memory_space_constraint(x, pltpu.VMEM) for x in (partial, filtered))
        return pl.pallas_call(
            write,
            out_shape=jax.ShapeDtypeStruct(state.shape, f32),
            in_specs=[vmem, vmem],
            out_specs=hbm,
            scratch_shapes=[pltpu.VMEM((5, PL_DEV, CELLS, 128), f32), dma((5,)), dma((4,))],
            compiler_params=pltpu.CompilerParams(vmem_limit_bytes=4 << 20),
        )(partial, filtered)

    return jax.shard_map(
        body,
        mesh=mesh,
        in_specs=(P(None, "gx", "az", None), P("gx", "az", None), P("gx"), P(), P(), P()),
        out_specs=P(None, "gx", "az", None),
        check_vma=False,
    )
```
